128 devices in a mesh: row: 8 (over y, core), col: 16 (over z, x).
Axes of the slice: x: 4, y: 4, z: 4, core: 2. Of those that a mesh axis runs over, the one named last changes fastest.
Arguments:
- wavefunction: bfloat16 [4096, 4096], P('row', 'col'), may hold values from -6 to 6
- left_env: bfloat16 [4, 4096, 4096], P(None, 'row'), may hold values from -0.09375 to 0.09375
- right_env: bfloat16 [4, 4096, 4096], P(None, None, 'col'), may hold values from -0.09375 to 0.09375
- filled_blocks: int32 [32, 32], replicated, may hold values 0 or 1
- term_columns: int32 [4, 32], replicated, may hold values 0 or 1
Outputs:
- product: bfloat16 [4096, 4096], P('row', 'col')
The draws below stay inside these ranges and needn't reach their ends.
All inputs are finite; a program needn't handle non-finite values.
Results may differ from the reference program's by a relative error of at most 0.001.
Values may be sent and summed in bfloat16 or wider, within the bound.
A program may use at most 128 MiB of HBM per device.

```python
import jax
import jax.numpy as jnp
from jax import lax

M = 4096
BLOCK = 128
TERMS = 4
NB = 32


def set_ends(drawn, stream_key, low, high):
    dims = drawn.shape
    spot = [jax.random.randint(jax.random.fold_in(stream_key, axis), (), 0, dims[axis]) for axis in range(len(dims))]
    drawn = drawn.at[tuple(spot)].set(low)
    longest = dims.index(max(dims))
    spot[longest] = (spot[longest] + 1) % dims[longest]
    return drawn.at[tuple(spot)].set(high)


def shard_levels(own_key, shape, split, low, largest):
    gain, own = 1.0, jax.random.fold_in(own_key, 6)
    for dim, shards_of in split:
        steps = jnp.exp(jax.random.uniform(jax.random.fold_in(own, dim), (shards_of,), jnp.float32, low / len(split), largest / len(split)))
        gain = gain * jnp.repeat(steps, shape[dim] // shards_of).reshape([-1 if axis == dim else 1 for axis in range(len(shape))])
    return gain


def scatter_about(stream_key, dims, deviation, limit, split=(), kind=jnp.bfloat16):
    entries = jax.random.normal(stream_key, dims, jnp.float32) * deviation
    if len(split) > 0:
        entries = shard_levels(stream_key, dims, split, -0.22, 0.18) * entries
    return jnp.clip(entries, min=-limit, max=limit).astype(kind)


def setup_inputs(seed: int = 0) -> dict:
    splits = jax.random.split(jax.random.key(seed), 6)
    wavefunction = scatter_about(splits[0], (M, M), 1.0, 6.0, ((0, 8), (1, 16)))
    left_env = scatter_about(splits[1], (TERMS, M, M), M ** -0.5, 0.09375, ((1, 8),))
    right_env = scatter_about(splits[2], (TERMS, M, M), M ** -0.5, 0.09375, ((2, 16),))
    filled_blocks = set_ends((jax.random.randint(splits[3], (NB, NB), 0, 8) < 3).astype(jnp.int32), jax.random.fold_in(splits[3], 1), 0, 1)
    term_columns = set_ends((jax.random.randint(splits[4], (TERMS, NB), 0, 4) < 3).astype(jnp.int32), jax.random.fold_in(splits[4], 1), 0, 1)
    return dict(wavefunction=wavefunction, left_env=left_env, right_env=right_env, filled_blocks=filled_blocks, term_columns=term_columns)


def reference(wavefunction, left_env, right_env, filled_blocks, term_columns):
    allowed = jnp.repeat(jnp.repeat(filled_blocks, BLOCK, axis=0), BLOCK, axis=1).astype(wavefunction.dtype)
    masked = wavefunction * allowed
    summed = jnp.zeros((M, M), jnp.float32)
    for term in range(TERMS):
        column_gate = jnp.repeat(term_columns[term], BLOCK).astype(left_env.dtype)
        acting = left_env[term] * column_gate[None, :]
        middle = jnp.dot(acting, masked, preferred_element_type=jnp.float32)
        summed = summed + jnp.dot(middle, right_env[term].astype(jnp.float32), precision=lax.Precision.HIGHEST, preferred_element_type=jnp.float32)
    return (summed * allowed.astype(jnp.float32)).astype(jnp.bfloat16)
```

```python
import functools

import jax
import jax.numpy as jnp
from jax import lax
from jax.experimental import pallas as pl
from jax.experimental.pallas import tpu as pltpu
from jax.sharding import PartitionSpec as P

BLOCK = 128
TERMS = 4
BANDS = 4
HALF = BLOCK // 2
COLS = 256
CODED = TERMS * BLOCK + 16
TOP = 32766.0
MESH = pl.DeviceIdType.MESH


def kernel(psi, left, right, cmask, omask, gates, out, buf_a, buf_b, psim, right_v, left_v, zbuf, acc,
           s_a1, r_a1, s_a2, r_a2, s_b1, r_b1, s_b2, r_b2, loc, s_z, r_z, s_load):
    row = lax.axis_index("row")
    col = lax.axis_index("col")
    y, c = row // 2, row % 2
    z, x = col // 4, col % 4
    d = 1 - 2 * c
    xf, xb = (x + d + 4) % 4, (x - d + 4) % 4
    zf, zb = (z + d + 4) % 4, (z - d + 4) % 4
    yf, yb, y2 = (y + d + 4) % 4, (y - d + 4) % 4, (y + 2) % 4
    dev_xf, dev_xb = (row, z * 4 + xf), (row, z * 4 + xb)
    dev_zf, dev_zb = (row, zf * 4 + x), (row, zb * 4 + x)
    dev_yf, dev_yb = (yf * 2 + c, col), (yb * 2 + c, col)
    dev_sib = (y * 2 + 1 - c, col)

    def remote(src, dst, send, recv, dev):
        return pltpu.make_async_remote_copy(
            src_ref=src, dst_ref=dst, send_sem=send, recv_sem=recv, device_id=dev, device_id_type=MESH)

    loads = [pltpu.make_async_copy(right, right_v, s_load.at[0]), pltpu.make_async_copy(left, left_v, s_load.at[1])]
    for load in loads:
        load.start()

    barrier = pltpu.get_barrier_semaphore()
    for dev in (dev_xf, dev_xb, dev_zf, dev_zb, dev_yf, dev_yb, dev_sib):
        pl.semaphore_signal(barrier, inc=1, device_id=dev, device_id_type=MESH)
    pl.semaphore_wait(barrier, 7)

    def own_a(p):
        return psi.at[pl.ds(pl.multiple_of(p * BLOCK, BLOCK), HALF), :]

    def own_b(p):
        return psi.at[pl.ds(pl.multiple_of(p * BLOCK + HALF, HALF), HALF), :]

    def a1(p, slot):
        if slot == 2:
            return remote(buf_a.at[p, z, xb], buf_a.at[p, z, xb], s_a1.at[p, 2], r_a1.at[p, 2], dev_xf)
        return remote(own_a(p), buf_a.at[p, z, x], s_a1.at[p, slot], r_a1.at[p, slot], (dev_xf, dev_xb)[slot])

    def b1(p, slot):
        if slot == 2:
            return remote(buf_b.at[p, x, zb], buf_b.at[p, x, zb], s_b1.at[p, 2], r_b1.at[p, 2], dev_zf)
        return remote(own_b(p), buf_b.at[p, x, z], s_b1.at[p, slot], r_b1.at[p, slot], (dev_zf, dev_zb)[slot])

    def a2(p, slot):
        src = buf_a.at[p, zb] if slot == 2 else buf_a.at[p, z]
        return remote(src, src, s_a2.at[p, slot], r_a2.at[p, slot], (dev_zf, dev_zb, dev_zf)[slot])

    def b2(p, slot):
        src = buf_b.at[p, xb] if slot == 2 else buf_b.at[p, x]
        return remote(src, src, s_b2.at[p, slot], r_b2.at[p, slot], (dev_xf, dev_xb, dev_xf)[slot])

    def local_a(p):
        return pltpu.make_async_copy(own_a(p), buf_a.at[p, z, x], loc.at[p, 0])

    def local_b(p):
        return pltpu.make_async_copy(own_b(p), buf_b.at[p, x, z], loc.at[p, 1])

    def first_send(p):
        for slot in (0, 1):
            a1(p, slot).start()
            b1(p, slot).start()
        local_a(p).start()
        local_b(p).start()

    def first_forward(p):
        a1(p, 0).wait_recv()
        a1(p, 2).start()
        b1(p, 0).wait_recv()
        b1(p, 2).start()

    def second_send(p):
        local_a(p).wait()
        local_b(p).wait()
        a1(p, 1).wait_recv()
        b1(p, 1).wait_recv()
        a1(p, 2).wait_recv()
        for slot in (0, 1):
            a2(p, slot).start()
        b1(p, 2).wait_recv()
        for slot in (0, 1):
            b2(p, slot).start()

    def second_forward(p):
        a2(p, 0).wait_recv()
        a2(p, 2).start()
        b2(p, 0).wait_recv()
        b2(p, 2).start()

    def second_wait(p):
        for slot in (1, 2):
            a2(p, slot).wait_recv()
            b2(p, slot).wait_recv()

    def z_copy(p, which):
        block = zbuf.at[(row, row, row, yb * 2 + c, yb * 2 + c, yf * 2 + c, y2 * 2 + c)[which], p]
        arrives = (2, 3, 1, 6, 4, 5, 7)[which]
        dev = (dev_yf, dev_yb, dev_sib, dev_yf, dev_sib, dev_sib, dev_sib)[which]
        return remote(block, block, s_z.at[p, which], r_z.at[p, arrives], dev)

    eye = lax.broadcasted_iota(jnp.int32, (BLOCK, BLOCK), 0) == lax.broadcasted_iota(jnp.int32, (BLOCK, BLOCK), 1)
    lines = lax.broadcasted_iota(jnp.int32, (16, BLOCK), 0)

    def make_z(p):
        for j in range(16):
            gate = cmask[p, :, j * COLS:(j + 1) * COLS]
            psim[:HALF, j * COLS:(j + 1) * COLS] = buf_a[p, j // 4, j % 4] * gate
            psim[HALF:, j * COLS:(j + 1) * COLS] = buf_b[p, j % 4, j // 4] * gate

        def term(t, scales):
            value = jnp.dot(psim[...], right_v[t], preferred_element_type=jnp.float32)
            top = jnp.maximum(jnp.max(jnp.abs(value), axis=1, keepdims=True), 1e-30)
            level = jnp.ceil(jnp.log2(top) * 256.0 + 0.05)
            code = jnp.round(value * (jnp.exp2(level * (-1.0 / 256.0)) * TOP))
            zbuf[row, p, pl.ds(pl.multiple_of(t * BLOCK, BLOCK), BLOCK), :] = code.astype(jnp.int32).astype(jnp.int16)
            line = jnp.sum(jnp.where(eye, level, 0.0), axis=0, keepdims=True)
            return jnp.where(lines == t, line, scales)

        scales = lax.fori_loop(0, TERMS, term, jnp.zeros((16, BLOCK), jnp.float32))
        zbuf[row, p, TERMS * BLOCK:, :BLOCK] = scales.astype(jnp.int32).astype(jnp.int16)
        zbuf[row, p, TERMS * BLOCK:, BLOCK:] = jnp.zeros((16, BLOCK), jnp.int16)

    def use_z(src, p):
        band = src * BANDS + p
        levels = zbuf[src, p, TERMS * BLOCK:, :BLOCK].astype(jnp.int32).astype(jnp.float32)
        high, low, factors = [], [], []
        for t in range(TERMS):
            scale = jnp.exp2(levels[t:t + 1, :] * (1.0 / 256.0)) * (gates[t, band].astype(jnp.float32) / TOP)
            scale = jnp.sum(jnp.where(eye, scale, 0.0), axis=1, keepdims=True)
            value = zbuf[src, p, t * BLOCK:(t + 1) * BLOCK, :].astype(jnp.int32).astype(jnp.float32) * scale
            top = value.astype(jnp.bfloat16)
            high.append(top)
            low.append((value - top.astype(jnp.float32)).astype(jnp.bfloat16))
            factors.append(left_v[t, :, pl.ds(pl.multiple_of(band * BLOCK, BLOCK), BLOCK)])
        acc[...] += jnp.dot(jnp.concatenate(factors + factors, axis=1), jnp.concatenate(high + low, axis=0),
                            preferred_element_type=jnp.float32)

    acc[...] = jnp.zeros_like(acc)
    first_send(0)
    first_send(1)
    first_forward(0)
    second_send(0)
    first_send(2)
    first_forward(1)
    second_send(1)
    first_send(3)
    loads[0].wait()

    def step(s, carry):
        @pl.when(s < BANDS)
        def _():
            second_forward(s)
            second_wait(s)
            make_z(s)
            for which in range(3):
                z_copy(s, which).start()

        @pl.when(s < BANDS - 2)
        def _():
            first_forward(s + 2)
            second_send(s + 2)

        @pl.when(s == 1)
        def _():
            loads[1].wait()

        def arrival(r, carry):
            late = jnp.where(r >= 7, 3, jnp.where(r >= 4, 2, 1))
            p = s - late

            @pl.when((p >= 0) & (p < BANDS))
            def _():
                @pl.when(r > 0)
                def _():
                    block = zbuf.at[0, 0]
                    remote(block, block, s_z.at[p, 0], r_z.at[p, r], dev_sib).wait_recv()

                @pl.when(r == 2)
                def _():
                    z_copy(p, 3).start()
                    z_copy(p, 4).start()

                @pl.when(r == 3)
                def _():
                    z_copy(p, 5).start()

                @pl.when(r == 6)
                def _():
                    z_copy(p, 6).start()

                y_of = jnp.where(r < 2, y, jnp.where(r >= 6, y2, jnp.where((r == 2) | (r == 5), yb, yf)))
                other = jnp.where((r == 1) | (r == 4) | (r == 5) | (r == 7), 1, 0)
                core = c + other * d
                use_z(y_of * 2 + core, p)

            return carry

        return lax.fori_loop(0, 8, arrival, carry)

    lax.fori_loop(0, BANDS + 3, step, 0)

    for i in range(4):
        out[i * BLOCK:(i + 1) * BLOCK, :] = (acc[i * BLOCK:(i + 1) * BLOCK, :] * omask[i]).astype(jnp.bfloat16)

    def drain(p, carry):
        for slot in range(3):
            for copy in (a1, b1, a2, b2):
                copy(p, slot).wait_send()
        for which in range(7):
            z_copy(p, which).wait_send()
        return carry

    lax.fori_loop(0, BANDS, drain, 0)


def on_device(wavefunction, left_env, right_env, filled_blocks, term_columns):
    row_place = lax.axis_index("row")
    col_place = lax.axis_index("col")
    filled_rows = lax.dynamic_slice(filled_blocks, (row_place * BANDS, 0), (BANDS, filled_blocks.shape[1]))
    cmask = jnp.repeat(filled_rows, BLOCK, axis=1).astype(jnp.bfloat16)[:, None, :]
    filled_here = lax.dynamic_slice(filled_rows, (0, col_place * 2), (BANDS, 2))
    omask = jnp.repeat(filled_here, BLOCK, axis=1).astype(jnp.float32)[:, None, :]
    any_space = pl.BlockSpec(memory_space=pl.ANY)
    vmem = pl.BlockSpec(memory_space=pltpu.VMEM)
    dma = pltpu.SemaphoreType.DMA
    return pl.pallas_call(
        kernel,
        out_shape=jax.ShapeDtypeStruct(wavefunction.shape, jnp.bfloat16),
        in_specs=[any_space, any_space, any_space, vmem, vmem, pl.BlockSpec(memory_space=pltpu.SMEM)],
        out_specs=vmem,
        scratch_shapes=[
            pltpu.VMEM((BANDS, 4, 4, HALF, COLS), jnp.bfloat16),
            pltpu.VMEM((BANDS, 4, 4, HALF, COLS), jnp.bfloat16),
            pltpu.VMEM((BLOCK, 4096), jnp.bfloat16),
            pltpu.VMEM((TERMS, 4096, COLS), jnp.bfloat16),
            pltpu.VMEM((TERMS, 512, 4096), jnp.bfloat16),
            pltpu.VMEM((8, BANDS, CODED, COLS), jnp.int16),
            pltpu.VMEM((512, COLS), jnp.float32),
        ] + [dma((BANDS, 3))] * 8 + [dma((BANDS, 2)), dma((BANDS, 7)), dma((BANDS, 8)), dma((2,))],
        compiler_params=pltpu.CompilerParams(
            collective_id=0, has_side_effects=True, vmem_limit_bytes=60 * 1024 * 1024),
    )(wavefunction, left_env, right_env, cmask, omask, term_columns)


def solution(mesh):
    in_specs = (P("row", "col"), P(None, "row", None), P(None, None, "col"), P(), P())
    return jax.shard_map(on_device, mesh=mesh, in_specs=in_specs, out_specs=P("row", "col"), check_vma=False)
```

```python
import functools

import jax
import jax.numpy as jnp
from jax import lax
from jax.experimental import pallas as pl
from jax.experimental.pallas import tpu as pltpu
from jax.sharding import PartitionSpec as P

BLOCK = 128
TERMS = 4
BANDS = 4
HALF = BLOCK // 2
COLS = 256
CODED = TERMS * BLOCK + 16
TOP = 32766.0
MESH = pl.DeviceIdType.MESH


def kernel(psi, left, right, filled, gates, out, buf_a, buf_b, psim, right_v, left_v, zbuf, acc,
           s_a1, r_a1, s_a2, r_a2, s_b1, r_b1, s_b2, r_b2, loc, s_z, r_z, s_load):
    row = lax.axis_index("row")
    col = lax.axis_index("col")
    y, c = row // 2, row % 2
    z, x = col // 4, col % 4
    d = 1 - 2 * c
    xf, xb = (x + d + 4) % 4, (x - d + 4) % 4
    zf, zb = (z + d + 4) % 4, (z - d + 4) % 4
    yf, yb, y2 = (y + d + 4) % 4, (y - d + 4) % 4, (y + 2) % 4
    dev_xf, dev_xb = (row, z * 4 + xf), (row, z * 4 + xb)
    dev_zf, dev_zb = (row, zf * 4 + x), (row, zb * 4 + x)
    dev_yf, dev_yb = (yf * 2 + c, col), (yb * 2 + c, col)
    dev_sib = (y * 2 + 1 - c, col)

    def remote(src, dst, send, recv, dev):
        return pltpu.make_async_remote_copy(
            src_ref=src, dst_ref=dst, send_sem=send, recv_sem=recv, device_id=dev, device_id_type=MESH)

    loads = [pltpu.make_async_copy(right, right_v, s_load.at[0]), pltpu.make_async_copy(left, left_v, s_load.at[1])]
    for p in range(BANDS):
        pltpu.make_async_copy(psi.at[pl.ds(p * BLOCK, HALF), :], buf_a.at[p, z, x], loc.at[p, 0]).start()
        pltpu.make_async_copy(psi.at[pl.ds(p * BLOCK + HALF, HALF), :], buf_b.at[p, x, z], loc.at[p, 1]).start()

    barrier = pltpu.get_barrier_semaphore()
    for dev in (dev_xf, dev_xb, dev_zf, dev_zb, dev_yf, dev_yb, dev_sib):
        pl.semaphore_signal(barrier, inc=1, device_id=dev, device_id_type=MESH)
    pl.semaphore_wait(barrier, 7)

    def a1(p, slot):
        if slot == 2:
            return remote(buf_a.at[p, z, xb], buf_a.at[p, z, xb], s_a1.at[p, 2], r_a1.at[p, 2], dev_xf)
        return remote(buf_a.at[p, z, x], buf_a.at[p, z, x], s_a1.at[p, slot], r_a1.at[p, slot], (dev_xf, dev_xb)[slot])

    def b1(p, slot):
        if slot == 2:
            return remote(buf_b.at[p, x, zb], buf_b.at[p, x, zb], s_b1.at[p, 2], r_b1.at[p, 2], dev_zf)
        return remote(buf_b.at[p, x, z], buf_b.at[p, x, z], s_b1.at[p, slot], r_b1.at[p, slot], (dev_zf, dev_zb)[slot])

    def a2(p, slot):
        src = buf_a.at[p, zb] if slot == 2 else buf_a.at[p, z]
        return remote(src, src, s_a2.at[p, slot], r_a2.at[p, slot], (dev_zf, dev_zb, dev_zf)[slot])

    def b2(p, slot):
        src = buf_b.at[p, xb] if slot == 2 else buf_b.at[p, x]
        return remote(src, src, s_b2.at[p, slot], r_b2.at[p, slot], (dev_xf, dev_xb, dev_xf)[slot])

    def first_send(p):
        own_a, own_b = psi.at[pl.ds(0, HALF), :], psi.at[pl.ds(HALF, HALF), :]
        pltpu.make_async_copy(own_a, buf_a.at[p, z, x], loc.at[p, 0]).wait()
        pltpu.make_async_copy(own_b, buf_b.at[p, x, z], loc.at[p, 1]).wait()
        for slot in (0, 1):
            a1(p, slot).start()
            b1(p, slot).start()

    def first_forward(p):
        a1(p, 0).wait_recv()
        a1(p, 2).start()
        b1(p, 0).wait_recv()
        b1(p, 2).start()

    def second_send(p):
        a1(p, 1).wait_recv()
        b1(p, 1).wait_recv()
        a1(p, 2).wait_recv()
        for slot in (0, 1):
            a2(p, slot).start()
        b1(p, 2).wait_recv()
        for slot in (0, 1):
            b2(p, slot).start()

    def second_forward(p):
        a2(p, 0).wait_recv()
        a2(p, 2).start()
        b2(p, 0).wait_recv()
        b2(p, 2).start()

    def second_wait(p):
        for slot in (1, 2):
            a2(p, slot).wait_recv()
            b2(p, slot).wait_recv()

    def z_copy(p, which):
        block = zbuf.at[(row, row, row, yb * 2 + c, yb * 2 + c, yf * 2 + c, y2 * 2 + c)[which], p]
        arrives = (2, 3, 1, 6, 4, 5, 7)[which]
        dev = (dev_yf, dev_yb, dev_sib, dev_yf, dev_sib, dev_sib, dev_sib)[which]
        return remote(block, block, s_z.at[p, which], r_z.at[p, arrives], dev)

    eye = lax.broadcasted_iota(jnp.int32, (BLOCK, BLOCK), 0) == lax.broadcasted_iota(jnp.int32, (BLOCK, BLOCK), 1)
    lines = lax.broadcasted_iota(jnp.int32, (16, BLOCK), 0)

    def make_z(p):
        for j in range(16):
            gate = jnp.concatenate([
                jnp.full((1, BLOCK), filled[row * BANDS + p, 2 * j + h].astype(jnp.float32)).astype(jnp.bfloat16)
                for h in range(2)], axis=1)
            psim[:HALF, j * COLS:(j + 1) * COLS] = buf_a[p, j // 4, j % 4] * gate
            psim[HALF:, j * COLS:(j + 1) * COLS] = buf_b[p, j % 4, j // 4] * gate

        def term(t, scales):
            value = jnp.dot(psim[...], right_v[t], preferred_element_type=jnp.float32)
            top = jnp.maximum(jnp.max(jnp.abs(value), axis=1, keepdims=True), 1e-30)
            level = jnp.ceil(jnp.log2(top) * 256.0 + 0.05)
            code = jnp.round(value * (jnp.exp2(level * (-1.0 / 256.0)) * TOP))
            zbuf[row, p, pl.ds(pl.multiple_of(t * BLOCK, BLOCK), BLOCK), :] = code.astype(jnp.int32).astype(jnp.int16)
            line = jnp.sum(jnp.where(eye, level, 0.0), axis=0, keepdims=True)
            return jnp.where(lines == t, line, scales)

        scales = lax.fori_loop(0, TERMS, term, jnp.zeros((16, BLOCK), jnp.float32))
        zbuf[row, p, TERMS * BLOCK:, :BLOCK] = scales.astype(jnp.int32).astype(jnp.int16)
        zbuf[row, p, TERMS * BLOCK:, BLOCK:] = jnp.zeros((16, BLOCK), jnp.int16)

    def use_z(src, p):
        band = src * BANDS + p
        levels = zbuf[src, p, TERMS * BLOCK:, :BLOCK].astype(jnp.int32).astype(jnp.float32)
        high, low, factors = [], [], []
        for t in range(TERMS):
            scale = jnp.exp2(levels[t:t + 1, :] * (1.0 / 256.0)) * (gates[t, band].astype(jnp.float32) / TOP)
            scale = jnp.sum(jnp.where(eye, scale, 0.0), axis=1, keepdims=True)
            value = zbuf[src, p, t * BLOCK:(t + 1) * BLOCK, :].astype(jnp.int32).astype(jnp.float32) * scale
            top = value.astype(jnp.bfloat16)
            high.append(top)
            low.append((value - top.astype(jnp.float32)).astype(jnp.bfloat16))
            factors.append(left_v[t, :, pl.ds(pl.multiple_of(band * BLOCK, BLOCK), BLOCK)])
        acc[...] += jnp.dot(jnp.concatenate(factors + factors, axis=1), jnp.concatenate(high + low, axis=0),
                            preferred_element_type=jnp.float32)

    first_send(0)
    first_send(1)
    loads[0].start()
    loads[1].start()
    acc[...] = jnp.zeros_like(acc)
    first_forward(0)
    second_send(0)
    first_forward(1)
    first_send(2)
    first_send(3)
    second_forward(0)
    second_send(1)
    first_forward(2)
    loads[0].wait()

    def step(s, carry):
        @pl.when(s < BANDS)
        def _():
            second_wait(s)
            make_z(s)
            for which in range(3):
                z_copy(s, which).start()

        @pl.when(s == 0)
        def _():
            loads[1].wait()

        @pl.when(s < BANDS - 1)
        def _():
            second_forward(s + 1)

        @pl.when(s < BANDS - 2)
        def _():
            second_send(s + 2)

        @pl.when(s < BANDS - 3)
        def _():
            first_forward(s + 3)

        def arrival(i, carry):
            r = jnp.where(i == 3, 1, jnp.where((i == 1) | (i == 2), i + 1, i))
            late = jnp.where((i == 0) | (i == 3), 0, jnp.where(i >= 6, 2, 1))
            p = s - late

            @pl.when((p >= 0) & (p < BANDS))
            def _():
                @pl.when(r > 0)
                def _():
                    block = zbuf.at[0, 0]
                    remote(block, block, s_z.at[p, 0], r_z.at[p, r], dev_sib).wait_recv()

                @pl.when(r == 2)
                def _():
                    z_copy(p, 3).start()
                    z_copy(p, 4).start()

                @pl.when(r == 3)
                def _():
                    z_copy(p, 5).start()

                @pl.when(r == 6)
                def _():
                    z_copy(p, 6).start()

                y_of = jnp.where(r < 2, y, jnp.where(r >= 6, y2, jnp.where((r == 2) | (r == 5), yb, yf)))
                other = jnp.where((r == 1) | (r == 4) | (r == 5) | (r == 7), 1, 0)
                core = c + other * d
                use_z(y_of * 2 + core, p)

            return carry

        return lax.fori_loop(0, 8, arrival, carry)

    lax.fori_loop(0, BANDS + 2, step, 0)

    for i in range(4):
        for h in range(2):
            keep = filled[row * BANDS + i, col * 2 + h].astype(jnp.float32)
            where = (slice(i * BLOCK, (i + 1) * BLOCK), slice(h * BLOCK, (h + 1) * BLOCK))
            out[where] = (acc[where] * keep).astype(jnp.bfloat16)

    def drain(p, carry):
        for slot in range(3):
            for copy in (a1, b1, a2, b2):
                copy(p, slot).wait_send()
        for which in range(7):
            z_copy(p, which).wait_send()
        return carry

    lax.fori_loop(0, BANDS, drain, 0)


def on_device(wavefunction, left_env, right_env, filled_blocks, term_columns):
    any_space = pl.BlockSpec(memory_space=pl.ANY)
    vmem = pl.BlockSpec(memory_space=pltpu.VMEM)
    smem = pl.BlockSpec(memory_space=pltpu.SMEM)
    dma = pltpu.SemaphoreType.DMA
    return pl.pallas_call(
        kernel,
        out_shape=jax.ShapeDtypeStruct(wavefunction.shape, jnp.bfloat16),
        in_specs=[any_space, any_space, any_space, smem, smem],
        out_specs=vmem,
        scratch_shapes=[
            pltpu.VMEM((BANDS, 4, 4, HALF, COLS), jnp.bfloat16),
            pltpu.VMEM((BANDS, 4, 4, HALF, COLS), jnp.bfloat16),
            pltpu.VMEM((BLOCK, 4096), jnp.bfloat16),
            pltpu.VMEM((TERMS, 4096, COLS), jnp.bfloat16),
            pltpu.VMEM((TERMS, 512, 4096), jnp.bfloat16),
            pltpu.VMEM((8, BANDS, CODED, COLS), jnp.int16),
            pltpu.VMEM((512, COLS), jnp.float32),
        ] + [dma((BANDS, 3))] * 8 + [dma((BANDS, 2)), dma((BANDS, 7)), dma((BANDS, 8)), dma((2,))],
        compiler_params=pltpu.CompilerParams(
            collective_id=0, has_side_effects=True, vmem_limit_bytes=60 * 1024 * 1024),
    )(wavefunction, left_env, right_env, filled_blocks, term_columns)


def solution(mesh):
    in_specs = (P("row", "col"), P(None, "row", None), P(None, None, "col"), P(), P())
    return jax.shard_map(on_device, mesh=mesh, in_specs=in_specs, out_specs=P("row", "col"), check_vma=False)
```

```python
import functools

import jax
import jax.numpy as jnp
from jax import lax
from jax.experimental import pallas as pl
from jax.experimental.pallas import tpu as pltpu
from jax.sharding import PartitionSpec as P

BLOCK = 128
TERMS = 4
COLS = 256
DEEP = 4096
TOP = 32766.0
MESH = pl.DeviceIdType.MESH
OWN = ((0, 64), (64, 64), (128, 128), (256, 128), (384, 128))
FAR = (4,)
GATHERS = [rows for _, rows in OWN] + [OWN[i][1] for i in FAR]
FAR_OF = {i: len(OWN) + f for f, i in enumerate(FAR)}
ORDER = (
    ("make", 0), ("make", 1), ("use", 0, 0), ("make", 2), ("take", 0, 2), ("take", 0, 3), ("use", 0, 1),
    ("use", 1, 0), ("take", 1, 2), ("take", 1, 3), ("use", 0, 2), ("use", 0, 3), ("use", 1, 1), ("make", 3),
    ("use", 0, 4), ("use", 0, 5), ("use", 2, 0), ("use", 2, 1), ("take", 2, 2), ("take", 2, 3), ("use", 1, 2),
    ("make", 4), ("take", 0, 6), ("take", 1, 6), ("use", 1, 3), ("use", 0, 6), ("use", 3, 0), ("use", 1, 4),
    ("use", 1, 5), ("use", 0, 7), ("make", 5), ("take", 3, 2), ("take", 3, 3), ("use", 3, 1), ("use", 2, 2),
    ("use", 2, 3), ("take", 2, 6), ("use", 3, 6), ("use", 1, 6), ("use", 2, 4), ("use", 2, 5), ("use", 3, 7),
    ("use", 1, 7), ("take", 4, 2), ("take", 4, 3), ("use", 3, 2), ("use", 3, 3), ("take", 3, 6), ("use", 2, 6),
    ("use", 3, 4), ("use", 3, 5), ("use", 2, 7),
)


def kernel(psi, left, right, filled, gates, out, *scratch):
    count = len(GATHERS)
    bufs_a, bufs_b = scratch[:count], scratch[count:2 * count]
    psim, right_v, left_v, z_small, z_large, acc, s_g, r_g, s_0, r_0, loc, s_z, r_z, s_load = scratch[2 * count:]
    row = lax.axis_index("row")
    col = lax.axis_index("col")
    y, c = row // 2, row % 2
    z, x = col // 4, col % 4
    d = 1 - 2 * c
    xf, xb, x2 = (x + d + 4) % 4, (x - d + 4) % 4, (x + 2) % 4
    zf, zb, z2 = (z + d + 4) % 4, (z - d + 4) % 4, (z + 2) % 4
    yf, yb, y2 = (y + d + 4) % 4, (y - d + 4) % 4, (y + 2) % 4
    dev_x = [(row, z * 4 + v) for v in (xf, xb, x2)]
    dev_z = [(row, v * 4 + x) for v in (zf, zb, z2)]
    dev_y = [(v * 2 + c, col) for v in (yf, yb, y2)]
    dev_sib = (y * 2 + 1 - c, col)

    def remote(src, dst, send, recv, dev):
        return pltpu.make_async_remote_copy(
            src_ref=src, dst_ref=dst, send_sem=send, recv_sem=recv, device_id=dev, device_id_type=MESH)

    loads = [pltpu.make_async_copy(right, right_v, s_load.at[0]), pltpu.make_async_copy(left, left_v, s_load.at[1])]

    def local(g):
        first, rows = OWN[g]
        half = rows // 2
        return (pltpu.make_async_copy(psi.at[pl.ds(first, half), :], bufs_a[g].at[z, x], loc.at[g, 0]),
                pltpu.make_async_copy(psi.at[pl.ds(first + half, half), :], bufs_b[g].at[x, z], loc.at[g, 1]))

    for g in range(len(OWN)):
        for copy in local(g):
            copy.start()

    barrier = pltpu.get_barrier_semaphore()
    partners = dev_x + dev_z + dev_y + [dev_sib]
    for dev in partners:
        pl.semaphore_signal(barrier, inc=1, device_id=dev, device_id_type=MESH)
    pl.semaphore_wait(barrier, len(partners))

    def one(g, slot):
        a, b = bufs_a[g].at[z, x], bufs_b[g].at[x, z]
        return (remote(a, a, s_g.at[g, slot], r_g.at[g, slot], dev_x[slot]),
                remote(b, b, s_g.at[g, 3 + slot], r_g.at[g, 3 + slot], dev_z[slot]))

    def two(g, slot):
        a, b = bufs_a[g].at[z], bufs_b[g].at[x]
        return (remote(a, a, s_g.at[g, 6 + slot], r_g.at[g, 6 + slot], dev_z[slot]),
                remote(b, b, s_g.at[g, 9 + slot], r_g.at[g, 9 + slot], dev_x[slot]))

    def far(f):
        i = FAR[f]
        g = FAR_OF[i]
        return (remote(bufs_a[i].at[z, x], bufs_a[g].at[z, x], s_0.at[f, 0], r_0.at[f, 0], dev_y[2]),
                remote(bufs_b[i].at[x, z], bufs_b[g].at[x, z], s_0.at[f, 1], r_0.at[f, 1], dev_y[2]))

    def send_one(g):
        if g >= len(OWN):
            for copy in far(g - len(OWN)):
                copy.wait_recv()
        for slot in range(3):
            for copy in one(g, slot):
                copy.start()

    def send_two(g):
        for slot in range(3):
            for copy in one(g, slot):
                copy.wait_recv()
        for slot in range(3):
            for copy in two(g, slot):
                copy.start()

    def wait_two(g):
        for slot in range(3):
            for copy in two(g, slot):
                copy.wait_recv()

    def coded(src, i):
        return z_small.at[src, i] if i < 2 else z_large.at[src, i - 2]

    def z_copy(i, which):
        block = coded((row, row, row, yb * 2 + c, yb * 2 + c, yf * 2 + c, y2 * 2 + c)[which], i)
        arrives = (2, 3, 1, 6, 4, 5, 7)[which]
        dev = (dev_y[0], dev_y[1], dev_sib, dev_y[0], dev_sib, dev_sib, dev_sib)[which]
        return remote(block, block, s_z.at[i, which], r_z.at[i, arrives], dev)

    def z_wait(i, r):
        block = coded(0, i)
        remote(block, block, s_z.at[i, 0], r_z.at[i, r], dev_sib).wait_recv()

    eye = lax.broadcasted_iota(jnp.int32, (BLOCK, BLOCK), 0) == lax.broadcasted_iota(jnp.int32, (BLOCK, BLOCK), 1)
    lines = lax.broadcasted_iota(jnp.int32, (16, BLOCK), 0)

    def make_z(g):
        i = g if g < len(OWN) else FAR[g - len(OWN)]
        src = row if g < len(OWN) else y2 * 2 + c
        rows = GATHERS[g]
        half = rows // 2
        sector = src * 4 + OWN[i][0] // BLOCK
        for j in range(16):
            gate = jnp.concatenate([
                jnp.full((1, BLOCK), filled[sector, 2 * j + h].astype(jnp.float32)).astype(jnp.bfloat16)
                for h in range(2)], axis=1)
            psim[:half, j * COLS:(j + 1) * COLS] = bufs_a[g][j // 4, j % 4] * gate
            psim[half:rows, j * COLS:(j + 1) * COLS] = bufs_b[g][j % 4, j // 4] * gate
        ref = coded(src, i)

        def term(t, scales):
            value = jnp.dot(psim[:rows], right_v[t], preferred_element_type=jnp.float32)
            top = jnp.maximum(jnp.max(jnp.abs(value), axis=1, keepdims=True), 1e-30)
            level = jnp.ceil(jnp.log2(top) * 256.0 + 0.05)
            code = jnp.round(value * (jnp.exp2(level * (-1.0 / 256.0)) * TOP))
            ref[pl.ds(pl.multiple_of(t * rows, rows), rows), :] = code.astype(jnp.int32).astype(jnp.int16)
            line = jnp.sum(jnp.where(eye[:rows], level, 0.0), axis=0, keepdims=True)
            return jnp.where(lines == t, line, scales)

        scales = lax.fori_loop(0, TERMS, term, jnp.zeros((16, BLOCK), jnp.float32), unroll=True)
        ref[TERMS * rows:, :BLOCK] = scales.astype(jnp.int32).astype(jnp.int16)
        ref[TERMS * rows:, BLOCK:] = jnp.zeros((16, BLOCK), jnp.int16)

    def use_z(src, sector, pieces, rows):
        band = src * 4 + sector
        high, low, factors = [], [], []
        levels = [piece[TERMS * rows:, :BLOCK].astype(jnp.int32).astype(jnp.float32) for piece in pieces]
        for t in range(TERMS):
            for piece, level in zip(pieces, levels):
                scale = jnp.exp2(level[t:t + 1, :] * (1.0 / 256.0)) * (gates[t, band].astype(jnp.float32) / TOP)
                scale = jnp.sum(jnp.where(eye[:rows], scale, 0.0), axis=1, keepdims=True)
                value = piece[t * rows:(t + 1) * rows, :].astype(jnp.int32).astype(jnp.float32) * scale
                top = value.astype(jnp.bfloat16)
                high.append(top)
                low.append((value - top.astype(jnp.float32)).astype(jnp.bfloat16))
            factors.append(left_v[t, :, pl.ds(pl.multiple_of(band * BLOCK, BLOCK), BLOCK)])
        acc[...] += jnp.dot(jnp.concatenate(factors + factors, axis=1), jnp.concatenate(high + low, axis=0),
                            preferred_element_type=jnp.float32)

    plan = []
    todo = []

    def act(function, *args):
        todo.append((function, args))

    def make(g):
        act(wait_two, g)
        act(make_z, g)
        if g < len(OWN):
            for which in range(3):
                act(lambda which: z_copy(g, which).start(), which)
        else:
            act(lambda: z_copy(FAR[g - len(OWN)], 6).start())
        if g == 0:
            act(send_two, 3)
            act(loads[1].wait)
            for later in range(4, len(GATHERS)):
                act(send_one, later)
        elif 2 <= g < len(GATHERS) - 2:
            act(send_two, g + 2)

    def take(i, r):
        act(z_wait, i, r)
        if r == 2 and i not in FAR_OF:
            act(lambda: z_copy(i, 3).start())
        if r in (2, 3, 6):
            act(lambda: z_copy(i, {2: 4, 3: 5, 6: 6}[r]).start())

    for name, *args in ORDER:
        if name == "make":
            make(*args)
        elif name == "take":
            take(*args)
        else:
            sector, r = args
            for i in ((0, 1), (2,), (3,), (4,))[sector]:
                if r in (1, 4, 5, 7):
                    act(z_wait, i, r)
            plan.append((list(todo), sector, r))
            todo.clear()
    assert len(plan) == 32 and len({entry[1:] for entry in plan}) == 32 and not todo

    for g in range(len(OWN)):
        for copy in local(g):
            copy.wait()
    for g in range(3):
        send_one(g)
    for f in range(len(FAR)):
        for copy in far(f):
            copy.start()
    loads[0].start()
    loads[1].start()
    acc[...] = jnp.zeros_like(acc)
    send_two(0)
    send_two(1)
    send_one(3)
    send_two(2)
    loads[0].wait()

    def step(u, carry):
        sector, r = 0, 0
        for n, (actions, sector_n, r_n) in enumerate(plan):
            if actions:
                @pl.when(u == n)
                def _(actions=actions):
                    for function, args in actions:
                        function(*args)
            sector = jnp.where(u == n, sector_n, sector)
            r = jnp.where(u == n, r_n, r)
        y_of = jnp.where(r < 2, y, jnp.where(r >= 6, y2, jnp.where((r == 2) | (r == 5), yb, yf)))
        other = jnp.where((r == 1) | (r == 4) | (r == 5) | (r == 7), 1, 0)
        src = y_of * 2 + c + other * d

        @pl.when(sector == 0)
        def _():
            use_z(src, 0, [z_small.at[src, 0], z_small.at[src, 1]], 64)

        @pl.when(sector > 0)
        def _():
            use_z(src, sector, [z_large.at[src, sector - 1]], BLOCK)

        return carry

    lax.fori_loop(0, len(plan), step, 0)

    for i in range(4):
        for h in range(2):
            keep = filled[row * 4 + i, col * 2 + h].astype(jnp.float32)
            where = (slice(i * BLOCK, (i + 1) * BLOCK), slice(h * BLOCK, (h + 1) * BLOCK))
            out[where] = (acc[where] * keep).astype(jnp.bfloat16)

    for g in range(count):
        for slot in range(3):
            for copy in one(g, slot) + two(g, slot):
                copy.wait_send()
    for f in range(len(FAR)):
        for copy in far(f):
            copy.wait_send()
    for i in range(len(OWN)):
        for which in range(7):
            if which != 3 or i not in FAR_OF:
                z_copy(i, which).wait_send()


def on_device(wavefunction, left_env, right_env, filled_blocks, term_columns):
    any_space = pl.BlockSpec(memory_space=pl.ANY)
    smem = pl.BlockSpec(memory_space=pltpu.SMEM)
    dma = pltpu.SemaphoreType.DMA
    count = len(GATHERS)
    halves = [pltpu.VMEM((4, 4, rows // 2, COLS), jnp.bfloat16) for rows in GATHERS]
    return pl.pallas_call(
        kernel,
        out_shape=jax.ShapeDtypeStruct(wavefunction.shape, jnp.bfloat16),
        in_specs=[any_space, any_space, any_space, smem, smem],
        out_specs=pl.BlockSpec(memory_space=pltpu.VMEM),
        scratch_shapes=halves + halves + [
            pltpu.VMEM((BLOCK, DEEP), jnp.bfloat16),
            pltpu.VMEM((TERMS, DEEP, COLS), jnp.bfloat16),
            pltpu.VMEM((TERMS, 512, DEEP), jnp.bfloat16),
            pltpu.VMEM((8, 2, TERMS * 64 + 16, COLS), jnp.int16),
            pltpu.VMEM((8, 3, TERMS * BLOCK + 16, COLS), jnp.int16),
            pltpu.VMEM((512, COLS), jnp.float32),
            dma((count, 12)), dma((count, 12)), dma((2, 2)), dma((2, 2)),
            dma((len(OWN), 2)), dma((len(OWN), 7)), dma((len(OWN), 8)), dma((2,)),
        ],
        compiler_params=pltpu.CompilerParams(
            collective_id=0, has_side_effects=True, vmem_limit_bytes=60 * 1024 * 1024),
    )(wavefunction, left_env, right_env, filled_blocks, term_columns)


def solution(mesh):
    in_specs = (P("row", "col"), P(None, "row", None), P(None, None, "col"), P(), P())
    return jax.shard_map(on_device, mesh=mesh, in_specs=in_specs, out_specs=P("row", "col"), check_vma=False)
```

```python
import functools

import jax
import jax.numpy as jnp
from jax import lax
from jax.experimental import pallas as pl
from jax.experimental.pallas import tpu as pltpu
from jax.sharding import PartitionSpec as P

BLOCK = 128
TERMS = 4
COLS = 256
DEEP = 4096
TOP = 32766.0
MESH = pl.DeviceIdType.MESH
OWN = ((0, 64), (64, 64), (128, 128), (256, 128), (384, 128))
FAR = (4,)
GATHERS = [rows for _, rows in OWN] + [OWN[i][1] for i in FAR]
FAR_OF = {i: len(OWN) + f for f, i in enumerate(FAR)}
ORDER = (
    ("make", 0), ("make", 1), ("use", 0, 0), ("use", 0, 1), ("make", 2), ("take", 0, 2), ("take", 0, 3),
    ("use", 1, 0), ("take", 1, 2), ("take", 1, 3), ("use", 0, 2), ("use", 0, 3), ("use", 1, 1), ("use", 0, 4),
    ("use", 0, 5), ("make", 3), ("use", 2, 0), ("use", 2, 1), ("take", 2, 2), ("take", 2, 3), ("use", 1, 2),
    ("use", 1, 3), ("make", 4), ("take", 0, 6), ("take", 1, 6), ("use", 0, 6), ("use", 1, 4), ("use", 1, 5),
    ("use", 3, 0), ("use", 3, 1), ("take", 3, 2), ("take", 3, 3), ("use", 0, 7), ("use", 2, 2), ("use", 2, 3),
    ("make", 5), ("take", 2, 6), ("use", 1, 6), ("use", 3, 6), ("use", 2, 4), ("use", 2, 5), ("use", 3, 7),
    ("use", 1, 7), ("take", 4, 2), ("take", 4, 3), ("use", 3, 2), ("use", 3, 3), ("take", 3, 6), ("use", 2, 6),
    ("use", 3, 4), ("use", 3, 5), ("use", 2, 7),
)


def kernel(psi, left, right, filled, gates, out, *scratch):
    count = len(GATHERS)
    bufs_a, bufs_b = scratch[:count], scratch[count:2 * count]
    psim, right_v, left_v, z_small, z_large, acc, s_g, r_g, s_0, r_0, loc, s_z, r_z, s_load = scratch[2 * count:]
    row = lax.axis_index("row")
    col = lax.axis_index("col")
    y, c = row // 2, row % 2
    z, x = col // 4, col % 4
    d = 1 - 2 * c
    xf, xb, x2 = (x + d + 4) % 4, (x - d + 4) % 4, (x + 2) % 4
    zf, zb, z2 = (z + d + 4) % 4, (z - d + 4) % 4, (z + 2) % 4
    yf, yb, y2 = (y + d + 4) % 4, (y - d + 4) % 4, (y + 2) % 4
    dev_x = [(row, z * 4 + v) for v in (xf, xb, x2)]
    dev_z = [(row, v * 4 + x) for v in (zf, zb, z2)]
    dev_y = [(v * 2 + c, col) for v in (yf, yb, y2)]
    dev_sib = (y * 2 + 1 - c, col)

    def remote(src, dst, send, recv, dev):
        return pltpu.make_async_remote_copy(
            src_ref=src, dst_ref=dst, send_sem=send, recv_sem=recv, device_id=dev, device_id_type=MESH)

    loads = [pltpu.make_async_copy(right, right_v, s_load.at[0]), pltpu.make_async_copy(left, left_v, s_load.at[1])]

    def local(g):
        first, rows = OWN[g]
        half = rows // 2
        return (pltpu.make_async_copy(psi.at[pl.ds(first, half), :], bufs_a[g].at[z, x], loc.at[g, 0]),
                pltpu.make_async_copy(psi.at[pl.ds(first + half, half), :], bufs_b[g].at[x, z], loc.at[g, 1]))

    for g in range(len(OWN)):
        for copy in local(g):
            copy.start()

    barrier = pltpu.get_barrier_semaphore()
    partners = dev_x + dev_z + dev_y + [dev_sib]
    for dev in partners:
        pl.semaphore_signal(barrier, inc=1, device_id=dev, device_id_type=MESH)
    pl.semaphore_wait(barrier, len(partners))

    def one(g, slot):
        a, b = bufs_a[g].at[z, x], bufs_b[g].at[x, z]
        return (remote(a, a, s_g.at[g, slot], r_g.at[g, slot], dev_x[slot]),
                remote(b, b, s_g.at[g, 3 + slot], r_g.at[g, 3 + slot], dev_z[slot]))

    def two(g, slot):
        a, b = bufs_a[g].at[z], bufs_b[g].at[x]
        return (remote(a, a, s_g.at[g, 6 + slot], r_g.at[g, 6 + slot], dev_z[slot]),
                remote(b, b, s_g.at[g, 9 + slot], r_g.at[g, 9 + slot], dev_x[slot]))

    def far(f):
        i = FAR[f]
        g = FAR_OF[i]
        return (remote(bufs_a[i].at[z, x], bufs_a[g].at[z, x], s_0.at[f, 0], r_0.at[f, 0], dev_y[2]),
                remote(bufs_b[i].at[x, z], bufs_b[g].at[x, z], s_0.at[f, 1], r_0.at[f, 1], dev_y[2]))

    def send_one(g):
        if g >= len(OWN):
            for copy in far(g - len(OWN)):
                copy.wait_recv()
        for slot in range(3):
            for copy in one(g, slot):
                copy.start()

    def send_two(g):
        for slot in range(3):
            for copy in one(g, slot):
                copy.wait_recv()
        for slot in range(3):
            for copy in two(g, slot):
                copy.start()

    def wait_two(g):
        for slot in range(3):
            for copy in two(g, slot):
                copy.wait_recv()

    def coded(src, i):
        return z_small.at[src, i] if i < 2 else z_large.at[src, i - 2]

    def z_copy(i, which):
        block = coded((row, row, row, yb * 2 + c, yb * 2 + c, yf * 2 + c, y2 * 2 + c)[which], i)
        arrives = (2, 3, 1, 6, 4, 5, 7)[which]
        dev = (dev_y[0], dev_y[1], dev_sib, dev_y[0], dev_sib, dev_sib, dev_sib)[which]
        return remote(block, block, s_z.at[i, which], r_z.at[i, arrives], dev)

    def z_wait(i, r):
        block = coded(0, i)
        remote(block, block, s_z.at[i, 0], r_z.at[i, r], dev_sib).wait_recv()

    eye = lax.broadcasted_iota(jnp.int32, (BLOCK, BLOCK), 0) == lax.broadcasted_iota(jnp.int32, (BLOCK, BLOCK), 1)
    lines = lax.broadcasted_iota(jnp.int32, (16, BLOCK), 0)

    def make_z(g):
        i = g if g < len(OWN) else FAR[g - len(OWN)]
        src = row if g < len(OWN) else y2 * 2 + c
        rows = GATHERS[g]
        half = rows // 2
        sector = src * 4 + OWN[i][0] // BLOCK
        for j in range(16):
            gate = jnp.concatenate([
                jnp.full((1, BLOCK), filled[sector, 2 * j + h].astype(jnp.float32)).astype(jnp.bfloat16)
                for h in range(2)], axis=1)
            psim[:half, j * COLS:(j + 1) * COLS] = bufs_a[g][j // 4, j % 4] * gate
            psim[half:rows, j * COLS:(j + 1) * COLS] = bufs_b[g][j % 4, j // 4] * gate
        ref = coded(src, i)

        def term(t, scales):
            value = jnp.dot(psim[:rows], right_v[t], preferred_element_type=jnp.float32)
            top = jnp.maximum(jnp.max(jnp.abs(value), axis=1, keepdims=True), 1e-30)
            level = jnp.ceil(jnp.log2(top) * 256.0 + 0.05)
            code = jnp.round(value * (jnp.exp2(level * (-1.0 / 256.0)) * TOP))
            ref[pl.ds(pl.multiple_of(t * rows, rows), rows), :] = code.astype(jnp.int32).astype(jnp.int16)
            line = jnp.sum(jnp.where(eye[:rows], level, 0.0), axis=0, keepdims=True)
            return jnp.where(lines == t, line, scales)

        scales = lax.fori_loop(0, TERMS, term, jnp.zeros((16, BLOCK), jnp.float32), unroll=True)
        ref[TERMS * rows:, :BLOCK] = scales.astype(jnp.int32).astype(jnp.int16)
        ref[TERMS * rows:, BLOCK:] = jnp.zeros((16, BLOCK), jnp.int16)

    def use_z(src, sector, pieces, rows):
        band = src * 4 + sector
        high, low, factors = [], [], []
        levels = [piece[TERMS * rows:, :BLOCK].astype(jnp.int32).astype(jnp.float32) for piece in pieces]
        for t in range(TERMS):
            for piece, level in zip(pieces, levels):
                scale = jnp.exp2(level[t:t + 1, :] * (1.0 / 256.0)) * (gates[t, band].astype(jnp.float32) / TOP)
                scale = jnp.sum(jnp.where(eye[:rows], scale, 0.0), axis=1, keepdims=True)
                value = piece[t * rows:(t + 1) * rows, :].astype(jnp.int32).astype(jnp.float32) * scale
                top = value.astype(jnp.bfloat16)
                high.append(top)
                low.append((value - top.astype(jnp.float32)).astype(jnp.bfloat16))
            factors.append(left_v[t, :, pl.ds(pl.multiple_of(band * BLOCK, BLOCK), BLOCK)])
        acc[...] += jnp.dot(jnp.concatenate(factors + factors, axis=1), jnp.concatenate(high + low, axis=0),
                            preferred_element_type=jnp.float32)

    plan = []
    todo = []

    def act(function, *args):
        todo.append((function, args))

    def make(g):
        act(wait_two, g)
        act(make_z, g)
        if g < len(OWN):
            for which in range(3):
                act(lambda which: z_copy(g, which).start(), which)
        else:
            act(lambda: z_copy(FAR[g - len(OWN)], 6).start())
        if g == 0:
            act(send_two, 3)
            act(loads[1].wait)
        if g == 1:
            act(send_one, 5)
        if g == 2:
            act(send_two, 4)
        if g == 3:
            act(send_two, 5)

    def take(i, r):
        act(z_wait, i, r)
        if r == 2 and i not in FAR_OF:
            act(lambda: z_copy(i, 3).start())
        if r in (2, 3, 6):
            act(lambda: z_copy(i, {2: 4, 3: 5, 6: 6}[r]).start())

    for name, *args in ORDER:
        if name == "make":
            make(*args)
        elif name == "take":
            take(*args)
        else:
            sector, r = args
            for i in ((0, 1), (2,), (3,), (4,))[sector]:
                if r in (1, 4, 5, 7):
                    act(z_wait, i, r)
            plan.append((list(todo), sector, r))
            todo.clear()
    assert len(plan) == 32 and len({entry[1:] for entry in plan}) == 32 and not todo

    for g in range(len(OWN)):
        for copy in local(g):
            copy.wait()
    for g in range(3):
        send_one(g)
    for f in range(len(FAR)):
        for copy in far(f):
            copy.start()
    loads[0].start()
    loads[1].start()
    acc[...] = jnp.zeros_like(acc)
    send_two(0)
    send_two(1)
    send_one(3)
    send_two(2)
    send_one(4)
    loads[0].wait()

    def step(u, carry):
        sector, r = 0, 0
        for n, (actions, sector_n, r_n) in enumerate(plan):
            if actions:
                @pl.when(u == n)
                def _(actions=actions):
                    for function, args in actions:
                        function(*args)
            sector = jnp.where(u == n, sector_n, sector)
            r = jnp.where(u == n, r_n, r)
        y_of = jnp.where(r < 2, y, jnp.where(r >= 6, y2, jnp.where((r == 2) | (r == 5), yb, yf)))
        other = jnp.where((r == 1) | (r == 4) | (r == 5) | (r == 7), 1, 0)
        src = y_of * 2 + c + other * d

        @pl.when(sector == 0)
        def _():
            use_z(src, 0, [z_small.at[src, 0], z_small.at[src, 1]], 64)

        @pl.when(sector > 0)
        def _():
            use_z(src, sector, [z_large.at[src, sector - 1]], BLOCK)

        return carry

    lax.fori_loop(0, len(plan), step, 0)

    for i in range(4):
        for h in range(2):
            keep = filled[row * 4 + i, col * 2 + h].astype(jnp.float32)
            where = (slice(i * BLOCK, (i + 1) * BLOCK), slice(h * BLOCK, (h + 1) * BLOCK))
            out[where] = (acc[where] * keep).astype(jnp.bfloat16)

    for g in range(count):
        for slot in range(3):
            for copy in one(g, slot) + two(g, slot):
                copy.wait_send()
    for f in range(len(FAR)):
        for copy in far(f):
            copy.wait_send()
    for i in range(len(OWN)):
        for which in range(7):
            if which != 3 or i not in FAR_OF:
                z_copy(i, which).wait_send()


def on_device(wavefunction, left_env, right_env, filled_blocks, term_columns):
    any_space = pl.BlockSpec(memory_space=pl.ANY)
    smem = pl.BlockSpec(memory_space=pltpu.SMEM)
    dma = pltpu.SemaphoreType.DMA
    count = len(GATHERS)
    halves = [pltpu.VMEM((4, 4, rows // 2, COLS), jnp.bfloat16) for rows in GATHERS]
    return pl.pallas_call(
        kernel,
        out_shape=jax.ShapeDtypeStruct(wavefunction.shape, jnp.bfloat16),
        in_specs=[any_space, any_space, any_space, smem, smem],
        out_specs=pl.BlockSpec(memory_space=pltpu.VMEM),
        scratch_shapes=halves + halves + [
            pltpu.VMEM((BLOCK, DEEP), jnp.bfloat16),
            pltpu.VMEM((TERMS, DEEP, COLS), jnp.bfloat16),
            pltpu.VMEM((TERMS, 512, DEEP), jnp.bfloat16),
            pltpu.VMEM((8, 2, TERMS * 64 + 16, COLS), jnp.int16),
            pltpu.VMEM((8, 3, TERMS * BLOCK + 16, COLS), jnp.int16),
            pltpu.VMEM((512, COLS), jnp.float32),
            dma((count, 12)), dma((count, 12)), dma((2, 2)), dma((2, 2)),
            dma((len(OWN), 2)), dma((len(OWN), 7)), dma((len(OWN), 8)), dma((2,)),
        ],
        compiler_params=pltpu.CompilerParams(
            collective_id=0, has_side_effects=True, vmem_limit_bytes=60 * 1024 * 1024),
    )(wavefunction, left_env, right_env, filled_blocks, term_columns)


def solution(mesh):
    in_specs = (P("row", "col"), P(None, "row", None), P(None, None, "col"), P(), P())
    return jax.shard_map(on_device, mesh=mesh, in_specs=in_specs, out_specs=P("row", "col"), check_vma=False)
```

```python
import functools

import jax
import jax.numpy as jnp
from jax import lax
from jax.experimental import pallas as pl
from jax.experimental.pallas import tpu as pltpu
from jax.sharding import PartitionSpec as P

BLOCK = 128
TERMS = 4
COLS = 256
DEEP = 4096
TOP = 32766.0
MESH = pl.DeviceIdType.MESH
OWN = ((0, 64), (64, 64), (128, 128), (256, 128), (384, 128))
FAR = (4,)
GATHERS = [rows for _, rows in OWN] + [OWN[i][1] for i in FAR]
FAR_OF = {i: len(OWN) + f for f, i in enumerate(FAR)}
ORDER = (
    ("make", 0), ("make", 1), ("use", 0, 0), ("use", 0, 1), ("make", 2), ("take", 0, 2), ("take", 0, 3),
    ("use", 1, 0), ("take", 1, 2), ("take", 1, 3), ("use", 0, 2), ("use", 0, 3), ("use", 1, 1), ("use", 0, 4),
    ("use", 0, 5), ("make", 3), ("use", 2, 0), ("use", 2, 1), ("take", 2, 2), ("take", 2, 3), ("use", 1, 2),
    ("use", 1, 3), ("make", 4), ("take", 0, 6), ("take", 1, 6), ("use", 0, 6), ("use", 1, 4), ("use", 1, 5),
    ("use", 3, 0), ("use", 3, 1), ("take", 3, 2), ("take", 3, 3), ("make", 5), ("use", 0, 7), ("use", 2, 2),
    ("use", 2, 3), ("take", 2, 6), ("use", 1, 6), ("use", 3, 6), ("use", 2, 4), ("use", 2, 5), ("use", 3, 7),
    ("use", 1, 7), ("take", 4, 2), ("take", 4, 3), ("use", 3, 2), ("use", 3, 3), ("take", 3, 6), ("use", 2, 6),
    ("use", 3, 4), ("use", 3, 5), ("use", 2, 7),
)


def kernel(psi, left, right, filled, gates, out, *scratch):
    count = len(GATHERS)
    bufs_a, bufs_b = scratch[:count], scratch[count:2 * count]
    psim, right_v, left_v, z_small, z_large, acc, s_g, r_g, s_0, r_0, loc, s_z, r_z, s_load = scratch[2 * count:]
    row = lax.axis_index("row")
    col = lax.axis_index("col")
    y, c = row // 2, row % 2
    z, x = col // 4, col % 4
    d = 1 - 2 * c
    xf, xb, x2 = (x + d + 4) % 4, (x - d + 4) % 4, (x + 2) % 4
    zf, zb, z2 = (z + d + 4) % 4, (z - d + 4) % 4, (z + 2) % 4
    yf, yb, y2 = (y + d + 4) % 4, (y - d + 4) % 4, (y + 2) % 4
    dev_x = [(row, z * 4 + v) for v in (xf, xb, x2)]
    dev_z = [(row, v * 4 + x) for v in (zf, zb, z2)]
    dev_y = [(v * 2 + c, col) for v in (yf, yb, y2)]
    dev_sib = (y * 2 + 1 - c, col)

    def remote(src, dst, send, recv, dev):
        return pltpu.make_async_remote_copy(
            src_ref=src, dst_ref=dst, send_sem=send, recv_sem=recv, device_id=dev, device_id_type=MESH)

    loads = [pltpu.make_async_copy(right, right_v, s_load.at[0]), pltpu.make_async_copy(left, left_v, s_load.at[1])]

    def local(g):
        first, rows = OWN[g]
        half = rows // 2
        return (pltpu.make_async_copy(psi.at[pl.ds(first, half), :], bufs_a[g].at[z, x], loc.at[g, 0]),
                pltpu.make_async_copy(psi.at[pl.ds(first + half, half), :], bufs_b[g].at[x, z], loc.at[g, 1]))

    for g in range(len(OWN)):
        for copy in local(g):
            copy.start()

    barrier = pltpu.get_barrier_semaphore()
    partners = dev_x + dev_z + dev_y + [dev_sib]
    for dev in partners:
        pl.semaphore_signal(barrier, inc=1, device_id=dev, device_id_type=MESH)
    pl.semaphore_wait(barrier, len(partners))

    def one(g, slot):
        a, b = bufs_a[g].at[z, x], bufs_b[g].at[x, z]
        return (remote(a, a, s_g.at[g, slot], r_g.at[g, slot], dev_x[slot]),
                remote(b, b, s_g.at[g, 3 + slot], r_g.at[g, 3 + slot], dev_z[slot]))

    def two(g, slot):
        a, b = bufs_a[g].at[z], bufs_b[g].at[x]
        return (remote(a, a, s_g.at[g, 6 + slot], r_g.at[g, 6 + slot], dev_z[slot]),
                remote(b, b, s_g.at[g, 9 + slot], r_g.at[g, 9 + slot], dev_x[slot]))

    def far(f):
        i = FAR[f]
        g = FAR_OF[i]
        return (remote(bufs_a[i].at[z, x], bufs_a[g].at[z, x], s_0.at[f, 0], r_0.at[f, 0], dev_y[2]),
                remote(bufs_b[i].at[x, z], bufs_b[g].at[x, z], s_0.at[f, 1], r_0.at[f, 1], dev_y[2]))

    def send_one(g):
        if g >= len(OWN):
            for copy in far(g - len(OWN)):
                copy.wait_recv()
        for slot in range(3):
            for copy in one(g, slot):
                copy.start()

    def send_two(g):
        for slot in range(3):
            for copy in one(g, slot):
                copy.wait_recv()
        for slot in range(3):
            for copy in two(g, slot):
                copy.start()

    def wait_two(g):
        for slot in range(3):
            for copy in two(g, slot):
                copy.wait_recv()

    def coded(src, i):
        return z_small.at[src, i] if i < 2 else z_large.at[src, i - 2]

    def z_copy(i, which):
        block = coded((row, row, row, yb * 2 + c, yb * 2 + c, yf * 2 + c, y2 * 2 + c)[which], i)
        arrives = (2, 3, 1, 6, 4, 5, 7)[which]
        dev = (dev_y[0], dev_y[1], dev_sib, dev_y[0], dev_sib, dev_sib, dev_sib)[which]
        return remote(block, block, s_z.at[i, which], r_z.at[i, arrives], dev)

    def z_wait(i, r):
        block = coded(0, i)
        remote(block, block, s_z.at[i, 0], r_z.at[i, r], dev_sib).wait_recv()

    eye = lax.broadcasted_iota(jnp.int32, (BLOCK, BLOCK), 0) == lax.broadcasted_iota(jnp.int32, (BLOCK, BLOCK), 1)
    lines = lax.broadcasted_iota(jnp.int32, (16, BLOCK), 0)

    def make_z(g):
        i = g if g < len(OWN) else FAR[g - len(OWN)]
        src = row if g < len(OWN) else y2 * 2 + c
        rows = GATHERS[g]
        half = rows // 2
        sector = src * 4 + OWN[i][0] // BLOCK
        for j in range(16):
            gate = jnp.concatenate([
                jnp.full((1, BLOCK), filled[sector, 2 * j + h].astype(jnp.float32)).astype(jnp.bfloat16)
                for h in range(2)], axis=1)
            psim[:half, j * COLS:(j + 1) * COLS] = bufs_a[g][j // 4, j % 4] * gate
            psim[half:rows, j * COLS:(j + 1) * COLS] = bufs_b[g][j % 4, j // 4] * gate
        ref = coded(src, i)

        def term(t, scales):
            value = jnp.dot(psim[:rows], right_v[t], preferred_element_type=jnp.float32)
            top = jnp.maximum(jnp.max(jnp.abs(value), axis=1, keepdims=True), 1e-30)
            level = jnp.ceil(jnp.log2(top) * 256.0 + 0.05)
            code = jnp.round(value * (jnp.exp2(level * (-1.0 / 256.0)) * TOP))
            ref[pl.ds(pl.multiple_of(t * rows, rows), rows), :] = code.astype(jnp.int32).astype(jnp.int16)
            line = jnp.sum(jnp.where(eye[:rows], level, 0.0), axis=0, keepdims=True)
            return jnp.where(lines == t, line, scales)

        scales = lax.fori_loop(0, TERMS, term, jnp.zeros((16, BLOCK), jnp.float32), unroll=True)
        ref[TERMS * rows:, :BLOCK] = scales.astype(jnp.int32).astype(jnp.int16)
        ref[TERMS * rows:, BLOCK:] = jnp.zeros((16, BLOCK), jnp.int16)

    def use_z(src, sector, pieces, rows):
        band = src * 4 + sector
        high, low, factors = [], [], []
        levels = [piece[TERMS * rows:, :BLOCK].astype(jnp.int32).astype(jnp.float32) for piece in pieces]
        for t in range(TERMS):
            for piece, level in zip(pieces, levels):
                scale = jnp.exp2(level[t:t + 1, :] * (1.0 / 256.0)) * (gates[t, band].astype(jnp.float32) / TOP)
                scale = jnp.sum(jnp.where(eye[:rows], scale, 0.0), axis=1, keepdims=True)
                value = piece[t * rows:(t + 1) * rows, :].astype(jnp.int32).astype(jnp.float32) * scale
                top = value.astype(jnp.bfloat16)
                high.append(top)
                low.append((value - top.astype(jnp.float32)).astype(jnp.bfloat16))
            factors.append(left_v[t, :, pl.ds(pl.multiple_of(band * BLOCK, BLOCK), BLOCK)])
        acc[...] += jnp.dot(jnp.concatenate(factors + factors, axis=1), jnp.concatenate(high + low, axis=0),
                            preferred_element_type=jnp.float32)

    plan = []
    todo = []

    def act(function, *args):
        todo.append((function, args))

    def make(g):
        act(wait_two, g)
        act(make_z, g)
        if g < len(OWN):
            for which in range(3):
                act(lambda which: z_copy(g, which).start(), which)
        else:
            act(lambda: z_copy(FAR[g - len(OWN)], 6).start())
        if g == 0:
            act(send_two, 3)
            act(loads[1].wait)
        if g == 1:
            act(send_one, 5)
        if g == 2:
            act(send_two, 4)
        if g == 3:
            act(send_two, 5)

    def take(i, r):
        act(z_wait, i, r)
        if r == 2 and i not in FAR_OF:
            act(lambda: z_copy(i, 3).start())
        if r in (2, 3, 6):
            act(lambda: z_copy(i, {2: 4, 3: 5, 6: 6}[r]).start())

    for name, *args in ORDER:
        if name == "make":
            make(*args)
        elif name == "take":
            take(*args)
        else:
            sector, r = args
            for i in ((0, 1), (2,), (3,), (4,))[sector]:
                if r in (1, 4, 5, 7):
                    act(z_wait, i, r)
            plan.append((list(todo), sector, r))
            todo.clear()
    assert len(plan) == 32 and len({entry[1:] for entry in plan}) == 32 and not todo

    for g in range(len(OWN)):
        for copy in local(g):
            copy.wait()
    for g in range(3):
        send_one(g)
    for f in range(len(FAR)):
        for copy in far(f):
            copy.start()
    loads[0].start()
    loads[1].start()
    acc[...] = jnp.zeros_like(acc)
    send_two(0)
    send_two(1)
    send_one(3)
    send_two(2)
    send_one(4)
    loads[0].wait()

    def step(u, carry):
        sector, r = 0, 0
        for n, (actions, sector_n, r_n) in enumerate(plan):
            if actions:
                @pl.when(u == n)
                def _(actions=actions):
                    for function, args in actions:
                        function(*args)
            sector = jnp.where(u == n, sector_n, sector)
            r = jnp.where(u == n, r_n, r)
        y_of = jnp.where(r < 2, y, jnp.where(r >= 6, y2, jnp.where((r == 2) | (r == 5), yb, yf)))
        other = jnp.where((r == 1) | (r == 4) | (r == 5) | (r == 7), 1, 0)
        src = y_of * 2 + c + other * d

        @pl.when(sector == 0)
        def _():
            use_z(src, 0, [z_small.at[src, 0], z_small.at[src, 1]], 64)

        @pl.when(sector > 0)
        def _():
            use_z(src, sector, [z_large.at[src, sector - 1]], BLOCK)

        return carry

    lax.fori_loop(0, len(plan), step, 0)

    for i in range(4):
        for h in range(2):
            keep = filled[row * 4 + i, col * 2 + h].astype(jnp.float32)
            where = (slice(i * BLOCK, (i + 1) * BLOCK), slice(h * BLOCK, (h + 1) * BLOCK))
            out[where] = (acc[where] * keep).astype(jnp.bfloat16)

    for g in range(count):
        for slot in range(3):
            for copy in one(g, slot) + two(g, slot):
                copy.wait_send()
    for f in range(len(FAR)):
        for copy in far(f):
            copy.wait_send()
    for i in range(len(OWN)):
        for which in range(7):
            if which != 3 or i not in FAR_OF:
                z_copy(i, which).wait_send()


def on_device(wavefunction, left_env, right_env, filled_blocks, term_columns):
    any_space = pl.BlockSpec(memory_space=pl.ANY)
    smem = pl.BlockSpec(memory_space=pltpu.SMEM)
    dma = pltpu.SemaphoreType.DMA
    count = len(GATHERS)
    halves = [pltpu.VMEM((4, 4, rows // 2, COLS), jnp.bfloat16) for rows in GATHERS]
    return pl.pallas_call(
        kernel,
        out_shape=jax.ShapeDtypeStruct(wavefunction.shape, jnp.bfloat16),
        in_specs=[any_space, any_space, any_space, smem, smem],
        out_specs=pl.BlockSpec(memory_space=pltpu.VMEM),
        scratch_shapes=halves + halves + [
            pltpu.VMEM((BLOCK, DEEP), jnp.bfloat16),
            pltpu.VMEM((TERMS, DEEP, COLS), jnp.bfloat16),
            pltpu.VMEM((TERMS, 512, DEEP), jnp.bfloat16),
            pltpu.VMEM((8, 2, TERMS * 64 + 16, COLS), jnp.int16),
            pltpu.VMEM((8, 3, TERMS * BLOCK + 16, COLS), jnp.int16),
            pltpu.VMEM((512, COLS), jnp.float32),
            dma((count, 12)), dma((count, 12)), dma((2, 2)), dma((2, 2)),
            dma((len(OWN), 2)), dma((len(OWN), 7)), dma((len(OWN), 8)), dma((2,)),
        ],
        compiler_params=pltpu.CompilerParams(
            collective_id=0, has_side_effects=True, vmem_limit_bytes=60 * 1024 * 1024),
    )(wavefunction, left_env, right_env, filled_blocks, term_columns)


def solution(mesh):
    in_specs = (P("row", "col"), P(None, "row", None), P(None, None, "col"), P(), P())
    return jax.shard_map(on_device, mesh=mesh, in_specs=in_specs, out_specs=P("row", "col"), check_vma=False)
```
